32 devices in a mesh: dp: 4 (over y, x), expert: 8 (over z, core).
Axes of the slice: x: 2, y: 2, z: 4, core: 2. Of those that a mesh axis runs over, the one named last changes fastest.
Arguments:
- images: bfloat16 [32, 197, 768], P(('dp', 'expert')), may hold values from -6 to 6
- ln1_gain: bfloat16 [768], P(('dp', 'expert')), may hold values from 0.25 to 1.75
- ln1_bias: bfloat16 [768], P(('dp', 'expert')), may hold values from -3 to 3
- qkv_weight: bfloat16 [768, 2304], P(('dp', 'expert')), may hold values from -0.21875 to 0.21875
- q_bias: bfloat16 [768], P(('dp', 'expert')), may hold values from -3 to 3
- v_bias: bfloat16 [768], P(('dp', 'expert')), may hold values from -3 to 3
- out_weight: bfloat16 [768, 768], P(('dp', 'expert')), may hold values from -0.875 to 0.875
- out_bias: bfloat16 [768], P(('dp', 'expert')), may hold values from -3 to 3
- ln2_gain: bfloat16 [768], P(('dp', 'expert')), may hold values from 0.25 to 1.75
- ln2_bias: bfloat16 [768], P(('dp', 'expert')), may hold values from -3 to 3
- in_weight: bfloat16 [8, 768, 3072], P('expert'), may hold values from -0.21875 to 0.21875
- in_bias: bfloat16 [8, 3072], P('expert'), may hold values from -3 to 3
- down_weight: bfloat16 [8, 3072, 768], P('expert'), may hold values from -0.109375 to 0.109375
- down_bias: bfloat16 [8, 768], P('expert'), may hold values from -3 to 3
- routes: int32 [32, 197, 2], P(('dp', 'expert')), may hold values from 0 to 7, all different within a row; in each aligned block of 197 rows (0 to 196, 197 to 393, ..., all dimensions but the last counted through in order) at most 50 rows name the same one
- gate_weights: float32 [32, 197, 2], P(('dp', 'expert')), may hold values from 0.1 to 1
- grad_out: bfloat16 [32, 197, 768], P(('dp', 'expert')), may hold values from -6 to 6
Outputs:
- block_output: bfloat16 [32, 197, 768], P(('dp', 'expert'))
- image_grad: float32 [32, 197, 768], P(('dp', 'expert'))
- ln1_gain_grad: float32 [768], P(('dp', 'expert'))
- ln1_bias_grad: float32 [768], P(('dp', 'expert'))
- qkv_weight_grad: float32 [768, 2304], P(('dp', 'expert'))
- q_bias_grad: float32 [768], P(('dp', 'expert'))
- v_bias_grad: float32 [768], P(('dp', 'expert'))
- out_weight_grad: float32 [768, 768], P(('dp', 'expert'))
- out_bias_grad: float32 [768], P(('dp', 'expert'))
- ln2_gain_grad: float32 [768], P(('dp', 'expert'))
- ln2_bias_grad: float32 [768], P(('dp', 'expert'))
- in_weight_grad: float32 [8, 768, 3072], P('expert', None, 'dp')
- in_bias_grad: float32 [8, 3072], P('expert', 'dp')
- down_weight_grad: float32 [8, 3072, 768], P('expert', 'dp')
- down_bias_grad: float32 [8, 768], P('expert', 'dp')
The draws below stay inside these ranges and needn't reach their ends.
Inputs may be any that keep to these rules, and one draw needn't show every extreme that they name: `routes`: in each aligned block of 197 rows (the tokens of one device) no expert is named more than 50 times, a bound that some block reaches; the two experts of a token differ.
All inputs are finite; a program needn't handle non-finite values.
Results may differ from the reference program's by a relative error of at most 0.012.
Values may be sent and summed in bfloat16 or wider, within the bound.
No kernel may reach another device: no remote copies, remote signals or barrier semaphores. Data moves between devices by JAX's collectives and lax.ppermute only.
A program may use at most 192 MiB of HBM per device.

```python
import math
import jax
import jax.numpy as jnp
import numpy as np
from jax import lax

D = 768
HEADS = 12
HEAD_DIM = 64
FF = 3072
SEQ = 197
IMG_DEV = 1
EXPERTS = 8
IMAGES = 32
CAP = 50
DEVICES = 32


def strengthened(values, key, source, target, blocks, factor):
    owner, partner = [(jnp.arange(values.shape[dim]) // (values.shape[dim] // blocks)).reshape([-1 if axis == dim else 1 for axis in range(values.ndim)]) for dim in (source, target)]
    chosen = jax.random.permutation(key, blocks)[partner]
    strong = (owner == chosen) | (owner == (partner + blocks // 2) % blocks)
    return jnp.where(strong, factor * values, values)


def block_scale(stream_key, extent, split, least, high):
    level = 1.0
    for position, blocks in split:
        draws = jax.random.uniform(jax.random.fold_in(jax.random.fold_in(stream_key, 6), position), (blocks,), jnp.float32, least / len(split), high / len(split))
        level = level * jnp.repeat(jnp.exp(draws), extent[position] // blocks).reshape((-1,) + (1,) * (len(extent) - 1 - position))
    return level


def routed_block(stream_key, own, number, rows, amount, top, bound, slope):
    ranking = jax.random.permutation(stream_key, amount)
    packed, common = portions_of(amount, rows * top, bound, slope, True), portions_of(amount, rows * top, bound, slope, False)
    places = jnp.arange(amount)

    def named(lengths, rotation):
        used = int((lengths > 0).sum())
        fixed = max(1, used // 4)
        moved = fixed + (places - fixed + rotation * (used - fixed)) % max(1, amount - fixed)
        return jnp.zeros((amount,), jnp.int32).at[ranking[jnp.where(places < fixed, places, moved)]].set(jnp.asarray(lengths, jnp.int32))

    lengths = jnp.where(number % 4 == 0, named(packed, number // 4), named(common, number - number // 4 - 1))
    mixed = jax.random.permutation(jax.random.fold_in(own, 3), amount)
    source_of, receiver = mixed[0:amount // 2 * 2:2], mixed[1:amount // 2 * 2:2]
    slack = jnp.minimum(lengths[source_of] - 1, bound - lengths[receiver]) // 2
    slack = jnp.where((source_of == ranking[0]) | (receiver == ranking[0]) | (lengths[receiver] == 0), 0, jnp.maximum(slack, 0))
    moved = jax.random.randint(jax.random.fold_in(own, 4), (amount // 2,), 0, 1 << 20) % (slack + 1)
    lengths = lengths.at[source_of].add(-moved).at[receiver].add(moved)
    members = jnp.searchsorted(jnp.cumsum(lengths), jnp.arange(rows * top), side="right").astype(jnp.int32)
    listing = members.reshape(top, rows).T
    listing = listing[jax.random.permutation(jax.random.fold_in(own, 1), rows)]
    rotation = jax.random.randint(jax.random.fold_in(own, 2), (rows, 1), 0, top)
    return jnp.take_along_axis(listing, (jnp.arange(top)[None, :] + rotation) % top, axis=1)


def portions_of(amount, total, limit, lean, full):
    weights = [(1 << 20) // math.isqrt(grade ** lean) + 1 for grade in range(1, amount + 1)]
    largest = limit if full else min(limit, max(-(-total // amount), total * weights[0] // sum(weights)))
    least = 1 if total - largest >= amount - 1 else 0
    given, rest = [largest] + [least] * (amount - 1), total - largest - least * (amount - 1)
    while rest > 0:
        movable = [i for i in range(1, amount) if given[i] < largest] or [i for i in range(1, amount) if given[i] < limit]
        mass, left = sum([weights[i] for i in movable]), rest
        for i in movable:
            extra = min(limit - given[i], max(1, left * weights[i] // mass), rest)
            given[i] = given[i] + extra
            rest = rest - extra
    return np.array(given)


def normal_values(own_key, dims, deviation, limit, split=(), kind=jnp.bfloat16):
    values = deviation * jax.random.normal(own_key, dims, jnp.float32)
    if split:
        values = values * block_scale(own_key, dims, split, -0.22, 0.18)
    return jnp.clip(values, -limit, limit).astype(kind)


def noise_with(rng, extent, width, reach, split, heavy, held_as=jnp.bfloat16):
    result = width * jax.random.normal(rng, extent, jnp.float32)
    if split:
        result = result * block_scale(rng, extent, split, -0.22, 0.18)
    return jnp.clip(strengthened(result, jax.random.fold_in(rng, 3), *heavy), -reach, reach).astype(held_as)


def setup_inputs(seed: int = 0) -> dict:
    streams_of = jax.random.split(jax.random.key(seed), 18)
    images = normal_values(streams_of[0], (IMAGES, SEQ, D), 1.0, 6.0, ((0, 32),))
    ln1_gain = jnp.clip(1.0 + 0.15 * jax.random.normal(streams_of[1], (D,), jnp.float32), 0.25, 1.75).astype(jnp.bfloat16)
    ln1_bias = normal_values(streams_of[2], (D,), 0.5, 3.0, ((0, 32),))
    qkv_weight = normal_values(streams_of[3], (D, 3 * D), D ** -0.5, 0.21875, ((0, 32),))
    q_bias = normal_values(streams_of[4], (D,), 0.5, 3.0, ((0, 32),))
    v_bias = normal_values(streams_of[5], (D,), 0.5, 3.0, ((0, 32),))
    out_weight = normal_values(streams_of[6], (D, D), (D // 16) ** -0.5, 0.875, ((0, 32),))
    out_bias = normal_values(streams_of[7], (D,), 0.5, 3.0, ((0, 32),))
    ln2_gain = jnp.clip(1.0 + 0.15 * jax.random.normal(streams_of[8], (D,), jnp.float32), 0.25, 1.75).astype(jnp.bfloat16)
    ln2_bias = normal_values(streams_of[9], (D,), 0.5, 3.0, ((0, 32),))
    in_weight = normal_values(streams_of[10], (EXPERTS, D, FF), D ** -0.5, 0.21875, ((0, 8),))
    in_bias = normal_values(streams_of[11], (EXPERTS, FF), 0.5, 3.0, ((0, 8),))
    down_weight = normal_values(streams_of[12], (EXPERTS, FF, D), FF ** -0.5, 0.109375, ((0, 8),))
    down_bias = normal_values(streams_of[13], (EXPERTS, D), 0.5, 3.0, ((0, 8),))
    routes_keys = jax.random.split(jax.random.fold_in(streams_of[14], 1), IMAGES * SEQ // (SEQ * IMG_DEV))
    routes_turns = jax.random.permutation(jax.random.fold_in(streams_of[14], 3), IMAGES * SEQ // (SEQ * IMG_DEV))
    routes = jax.vmap(lambda own, number: routed_block(jax.random.fold_in(streams_of[14], 2), own, number, SEQ * IMG_DEV, EXPERTS, 2, CAP, 0))(routes_keys, routes_turns).reshape((IMAGES, SEQ, 2))
    gate_weights = jnp.clip(0.1 + 0.9 * jax.random.uniform(streams_of[15], (IMAGES, SEQ, 2), jnp.float32) ** block_scale(streams_of[15], (IMAGES, SEQ, 2), ((0, 32),), -0.2, 0.2), 0.1, 1.0)
    grad_out = noise_with(streams_of[16], (IMAGES, SEQ, D), 1.0, 6.0, ((0, 32),), (0, 2, 32, 2.75))
    return {"images": images, "ln1_gain": ln1_gain, "ln1_bias": ln1_bias, "qkv_weight": qkv_weight, "q_bias": q_bias, "v_bias": v_bias, "out_weight": out_weight, "out_bias": out_bias, "ln2_gain": ln2_gain, "ln2_bias": ln2_bias, "in_weight": in_weight, "in_bias": in_bias, "down_weight": down_weight, "down_bias": down_bias, "routes": routes, "gate_weights": gate_weights, "grad_out": grad_out}


EPSILON = 1e-06

def to_half(values):
    return lax.optimization_barrier(values.astype(jnp.bfloat16))

def layer_norm(values, gain, shift):
    average = lax.optimization_barrier(jnp.mean(values, axis=-1, keepdims=True))
    centred = values - average
    inverse = lax.rsqrt(lax.optimization_barrier(jnp.mean(centred * centred, axis=-1, keepdims=True)) + EPSILON)
    normal = centred * inverse
    return (normal * gain.astype(jnp.float32) + shift.astype(jnp.float32), normal, inverse)

def norm_back(upstream, normal, inverse, gain):
    weighted = upstream * gain.astype(jnp.float32)
    first_mean = lax.optimization_barrier(jnp.mean(weighted, axis=-1, keepdims=True))
    second_mean = lax.optimization_barrier(jnp.mean(weighted * normal, axis=-1, keepdims=True))
    return inverse * (weighted - first_mean - normal * second_mean)

def slot_positions(flat_routes, expert_count, capacity):
    onehot = (flat_routes[:, None] == jnp.arange(expert_count, dtype=jnp.int32)[None, :]).astype(jnp.int32)
    earlier = jnp.cumsum(onehot, axis=0) - onehot
    return (flat_routes * capacity + lax.optimization_barrier(jnp.sum(earlier * onehot, axis=1))).astype(jnp.int32)

def split_heads(qkv_image):
    parts = qkv_image.astype(jnp.float32).reshape(SEQ, 3, HEADS, HEAD_DIM)
    return (parts[:, 0], parts[:, 1], parts[:, 2])

def head_scores(queries, key_heads):
    return jnp.einsum('qhd,khd->hqk', queries, key_heads) * HEAD_DIM ** (-0.5)

def attend(qkv_image):
    queries, key_heads, value_heads = split_heads(qkv_image)
    scores = head_scores(queries, key_heads)
    log_total = jnp.log(lax.optimization_barrier(jnp.sum(jnp.exp(scores), axis=-1, keepdims=True)))
    attention = to_half(jnp.exp(scores - log_total)).astype(jnp.float32)
    context = jnp.einsum('hqk,khd->qhd', attention, value_heads)
    return (context.reshape(SEQ, D).astype(jnp.bfloat16), log_total)

def attend_back(operands):
    qkv_image, log_total, upstream = operands
    queries, key_heads, value_heads = split_heads(qkv_image)
    probable = jnp.exp(head_scores(queries, key_heads) - log_total)
    attention = to_half(probable).astype(jnp.float32)
    incoming = upstream.astype(jnp.float32).reshape(SEQ, HEADS, HEAD_DIM)
    grad_values = jnp.einsum('hqk,qhd->khd', attention, incoming)
    grad_probs = jnp.einsum('qhd,khd->hqk', incoming, value_heads)
    centre = lax.optimization_barrier(jnp.sum(probable * grad_probs, axis=-1, keepdims=True))
    grad_scores = to_half(probable * (grad_probs - centre) * HEAD_DIM ** (-0.5)).astype(jnp.float32)
    grad_queries = jnp.einsum('hqk,khd->qhd', grad_scores, key_heads)
    grad_keys = jnp.einsum('hqk,qhd->khd', grad_scores, queries)
    return jnp.stack([grad_queries, grad_keys, grad_values], axis=1).reshape(SEQ, 3 * D)

def expert_forward(operands):
    weight_in, bias_in, weight_down, bias_down, inputs = operands
    hidden_pre = jnp.dot(inputs, weight_in, preferred_element_type=jnp.float32) + bias_in.astype(jnp.float32)
    activated = to_half(jax.nn.gelu(hidden_pre))
    return to_half(jnp.dot(activated, weight_down, preferred_element_type=jnp.float32) + bias_down.astype(jnp.float32))

def expert_backward(operands):
    weight_in, bias_in, weight_down, inputs, upstream = operands
    hidden_pre = jnp.dot(inputs, weight_in, preferred_element_type=jnp.float32) + bias_in.astype(jnp.float32)
    activated = to_half(jax.nn.gelu(hidden_pre))
    grad_hidden = jnp.dot(upstream, weight_down.T, preferred_element_type=jnp.float32)
    grad_pre = to_half(jax.vjp(jax.nn.gelu, hidden_pre)[1](grad_hidden)[0])
    grad_weight_down = jnp.dot(activated.T, upstream, preferred_element_type=jnp.float32)
    grad_bias_down = lax.optimization_barrier(jnp.sum(upstream.astype(jnp.float32), axis=0))
    grad_weight_in = jnp.dot(inputs.T, grad_pre, preferred_element_type=jnp.float32)
    grad_bias_in = lax.optimization_barrier(jnp.sum(grad_pre.astype(jnp.float32), axis=0))
    grad_inputs = to_half(jnp.dot(grad_pre, weight_in.T, preferred_element_type=jnp.float32))
    return (grad_inputs, grad_weight_in, grad_bias_in, grad_weight_down, grad_bias_down)

def reference(images, ln1_gain, ln1_bias, qkv_weight, q_bias, v_bias, out_weight, out_bias, ln2_gain, ln2_bias, in_weight, in_bias, down_weight, down_bias, routes, gate_weights, grad_out):
    token_total = IMAGES * SEQ
    per_device = SEQ * IMG_DEV
    inputs = images.reshape(token_total, D).astype(jnp.float32)
    normed_one, normal_one, inverse_one = layer_norm(inputs, ln1_gain, ln1_bias)
    normed_one = to_half(normed_one)
    bias_row = jnp.concatenate([q_bias.astype(jnp.float32), jnp.zeros((D,), jnp.float32), v_bias.astype(jnp.float32)])
    projected = to_half(jnp.dot(normed_one, qkv_weight, preferred_element_type=jnp.float32) + bias_row)
    context, log_totals = lax.map(attend, projected.reshape(IMAGES, SEQ, 3 * D))
    context = context.reshape(token_total, D)
    residual = inputs + jnp.dot(context, out_weight, preferred_element_type=jnp.float32) + out_bias.astype(jnp.float32)
    normed_two, normal_two, inverse_two = layer_norm(residual, ln2_gain, ln2_bias)
    normed_two = to_half(normed_two)
    flat_routes = routes.reshape(DEVICES, 2 * per_device)
    positions = jax.vmap(lambda block_routes: slot_positions(block_routes, EXPERTS, CAP))(flat_routes)
    mixing = gate_weights.reshape(DEVICES, 2 * per_device, 1).astype(jnp.float32)

    def dispatch(device_rows):
        filled = jax.vmap(lambda slots_here, source: jnp.zeros((EXPERTS * CAP, D), device_rows.dtype).at[slots_here].set(source))(positions, device_rows)
        return filled.reshape(DEVICES, EXPERTS, CAP, D).transpose(1, 0, 2, 3).reshape(EXPERTS, DEVICES * CAP, D)

    def collect(expert_rows):
        returned = expert_rows.reshape(EXPERTS, DEVICES, CAP, D).transpose(1, 0, 2, 3).reshape(DEVICES, EXPERTS * CAP, D)
        return jax.vmap(lambda buffer_rows, slots_here: buffer_rows[slots_here])(returned, positions)
    expert_inputs = dispatch(jnp.repeat(normed_two.reshape(DEVICES, per_device, D), 2, axis=1))
    expert_outputs = lax.map(expert_forward, (in_weight, in_bias, down_weight, down_bias, expert_inputs))
    picked = collect(expert_outputs).astype(jnp.float32)
    mixture = lax.optimization_barrier(jnp.sum((picked * mixing).reshape(DEVICES, per_device, 2, D), axis=2)).reshape(token_total, D)
    block_output = (residual + mixture).astype(jnp.bfloat16).reshape(IMAGES, SEQ, D)
    upstream = grad_out.reshape(token_total, D).astype(jnp.float32)
    routed_grads = to_half(jnp.repeat(upstream.reshape(DEVICES, per_device, D), 2, axis=1) * mixing)
    grad_inputs, in_weight_grad, in_bias_grad, down_weight_grad, down_bias_grad = lax.map(expert_backward, (in_weight, in_bias, down_weight, expert_inputs, dispatch(routed_grads)))
    grad_normed_two = lax.optimization_barrier(jnp.sum(collect(grad_inputs).astype(jnp.float32).reshape(DEVICES, per_device, 2, D), axis=2)).reshape(token_total, D)
    ln2_gain_grad = lax.optimization_barrier(jnp.sum(grad_normed_two * normal_two, axis=0))
    ln2_bias_grad = lax.optimization_barrier(jnp.sum(grad_normed_two, axis=0))
    grad_residual = upstream + norm_back(grad_normed_two, normal_two, inverse_two, ln2_gain)
    out_bias_grad = lax.optimization_barrier(jnp.sum(grad_residual, axis=0))
    branch_grad = to_half(grad_residual)
    out_weight_grad = jnp.dot(context.T, branch_grad, preferred_element_type=jnp.float32)
    grad_context = to_half(jnp.dot(branch_grad, out_weight.T, preferred_element_type=jnp.float32))
    grad_projected = lax.map(attend_back, (projected.reshape(IMAGES, SEQ, 3 * D), log_totals, grad_context.reshape(IMAGES, SEQ, D))).reshape(token_total, 3 * D)
    q_bias_grad = lax.optimization_barrier(jnp.sum(grad_projected[:, :D], axis=0))
    v_bias_grad = lax.optimization_barrier(jnp.sum(grad_projected[:, 2 * D:], axis=0))
    projected_grad = to_half(grad_projected)
    qkv_weight_grad = jnp.dot(normed_one.T, projected_grad, preferred_element_type=jnp.float32)
    grad_normed_one = jnp.dot(projected_grad, qkv_weight.T, preferred_element_type=jnp.float32)
    ln1_gain_grad = lax.optimization_barrier(jnp.sum(grad_normed_one * normal_one, axis=0))
    ln1_bias_grad = lax.optimization_barrier(jnp.sum(grad_normed_one, axis=0))
    image_grad = (grad_residual + norm_back(grad_normed_one, normal_one, inverse_one, ln1_gain)).reshape(IMAGES, SEQ, D)
    return (block_output, image_grad, ln1_gain_grad, ln1_bias_grad, qkv_weight_grad, q_bias_grad, v_bias_grad, out_weight_grad, out_bias_grad, ln2_gain_grad, ln2_bias_grad, in_weight_grad, in_bias_grad, down_weight_grad, down_bias_grad)
```

```python
import jax
import jax.numpy as jnp
import numpy as np
from jax import lax
from jax.sharding import PartitionSpec as P

HEAD_DIM = 64
EPSILON = 1e-06
BOTH = ("dp", "expert")
F32 = jnp.float32
BF16 = jnp.bfloat16


def to_half(values):
    return lax.optimization_barrier(values.astype(BF16))


def dot(left, right):
    return jnp.dot(left, right, preferred_element_type=F32)


def dot_t(left, right):
    return lax.dot_general(left, right, (((0,), (0,)), ((), ())), preferred_element_type=F32)


def dot_nt(left, right):
    return lax.dot_general(left, right, (((1,), (1,)), ((), ())), preferred_element_type=F32)


def normalize(values):
    average = jnp.mean(values, axis=-1, keepdims=True)
    centred = values - average
    inverse = lax.rsqrt(jnp.mean(centred * centred, axis=-1, keepdims=True) + EPSILON)
    return centred * inverse, inverse


def norm_back(upstream, normal, inverse, gain):
    weighted = upstream * gain
    first_mean = jnp.mean(weighted, axis=-1, keepdims=True)
    second_mean = jnp.mean(weighted * normal, axis=-1, keepdims=True)
    return inverse * (weighted - first_mean - normal * second_mean)


class Links:
    def __init__(self, dp_size, expert_size):
        self.total = dp_size * expert_size
        self.bits = self.total.bit_length() - 1
        self.dp_bits = dp_size.bit_length() - 1
        self.expert_size = expert_size
        plain = list(range(1, self.bits))
        turned = plain[:-2] + [plain[-1], plain[-2]]
        self.orders = (plain, turned)
        self.me = lax.axis_index("dp") * expert_size + lax.axis_index("expert")
        self.core = self.me % 2

    def swap(self, values, masks):
        pairs = [(i, i ^ masks[i % 2]) for i in range(self.total)]
        return lax.ppermute(values, BOTH, pairs)

    def core_swap(self, values):
        return self.swap(values, (1, 1))

    def stage(self, values, k):
        return self.swap(values, (1 << self.orders[0][k], 1 << self.orders[1][k]))

    def owners(self, rows):
        half = self.total // 2
        tables = []
        for core in (0, 1):
            table = []
            for flip in (0, 1):
                order = self.orders[core ^ flip]
                for q in range(half):
                    device = flip
                    for k, bit in enumerate(order):
                        device ^= ((q >> k) & 1) << bit
                    table.append(device)
            tables.append(np.repeat(np.array(table, np.int32), rows))
        inner = np.tile(np.arange(rows, dtype=np.int32), self.total)
        offset = jnp.where(self.core == 0, jnp.asarray(tables[0]), jnp.asarray(tables[1]))
        return (offset ^ self.me) * rows + jnp.asarray(inner)

    def gather(self, block):
        last = self.bits - 1
        held = block
        for k in range(last - 2):
            held = jnp.concatenate([held, self.stage(held, k)])
        pieces = [held]
        for k in range(last - 2, last):
            pieces = pieces + [self.stage(piece, k) for piece in pieces]
        others = [self.core_swap(piece) for piece in pieces]
        return jnp.concatenate(pieces + others)

    def scatter_sum(self, kept, sent):
        total = kept + self.core_swap(sent).astype(F32)
        for k in range(self.bits - 2, -1, -1):
            half = total.shape[0] // 2
            moved = self.stage(total[half:].astype(BF16), k)
            total = total[:half] + moved.astype(F32)
        return total

    def gather_dp(self, values):
        base = self.bits - self.dp_bits - 1
        pieces = [values]
        for k in range(base, self.bits - 1):
            pieces = pieces + [self.stage(piece, k) for piece in pieces]
        return jnp.concatenate(pieces)

    def exchange(self, values, chunk):
        groups = self.expert_size // 2
        parts = [values[:chunk]]
        for k in range(1, groups):
            parts.append(self.swap(values[k * chunk : (k + 1) * chunk], (2 * k, 2 * k)))
        return jnp.concatenate(parts)


def head_scores(queries, key_heads):
    return (
        jnp.einsum("qhd,khd->hqk", queries, key_heads, preferred_element_type=F32)
        * HEAD_DIM ** (-0.5)
    )


def per_device(
    images,
    ln1_gain,
    ln1_bias,
    qkv_weight,
    q_bias,
    v_bias,
    out_weight,
    out_bias,
    ln2_gain,
    ln2_bias,
    in_weight,
    in_bias,
    down_weight,
    down_bias,
    routes,
    gate_weights,
    grad_out,
):
    links = Links(lax.axis_size("dp"), lax.axis_size("expert"))
    expert_count = links.expert_size
    width = images.shape[-1]
    tokens = images.shape[0] * images.shape[1]
    heads = width // HEAD_DIM
    rows = qkv_weight.shape[0]

    vectors = jnp.stack([ln1_gain, ln1_bias, q_bias, v_bias, out_bias, ln2_gain, ln2_bias], axis=1)
    vectors = jnp.pad(vectors, ((0, 0), (0, 128 - vectors.shape[1])))
    first_rel = links.gather(jnp.concatenate([vectors, qkv_weight], axis=1))
    out_rel = links.gather(out_weight)
    places = links.owners(rows)
    select = (places[:, None] == jnp.arange(width, dtype=jnp.int32)[None, :]).astype(BF16)
    qkv_rel = first_rel[:, 128:]
    vector_rows = dot_t(first_rel[:, :128], select)
    gain_one, bias_one, full_q_bias, full_v_bias, full_out_bias, gain_two, bias_two = (
        vector_rows[i : i + 1] for i in range(7)
    )

    limit = max(2, -(-2 * tokens // expert_count))
    room = -(-limit // 4) * 4
    chunk = 2 * room
    slots = chunk * (expert_count // 2)
    table = jnp.concatenate(
        [
            routes.reshape(tokens, 2).astype(F32).T,
            gate_weights.reshape(tokens, 2).T,
        ]
    )
    tables = (table, links.core_swap(table))
    upper = (
        jnp.arange(tokens)[:, None] < jnp.arange(tokens)[None, :]
    ).astype(BF16)
    experts = jnp.arange(expert_count, dtype=jnp.int32)[:, None]
    slot_ids = jnp.arange(slots, dtype=jnp.int32)[:, None]
    group = lax.axis_index("expert") // 2
    picks, mixes = [], []
    slot_gate = jnp.zeros((slots, 1), F32)
    for which, entry in enumerate(tables):
        named = entry[:2].astype(jnp.int32)
        onehot = [named[c : c + 1] == experts for c in (0, 1)]
        earlier = dot((onehot[0] | onehot[1]).astype(BF16), upper)
        hit, gate = [], entry[2:]
        for c in (0, 1):
            rank = jnp.sum(jnp.where(onehot[c], earlier, 0.0), axis=0, keepdims=True)
            route = named[c : c + 1]
            place = ((route // 2) ^ group) * chunk + which * room + rank.astype(jnp.int32)
            place = jnp.where(route % 2 == links.core, place, -1)
            hit.append(slot_ids == place)
        picks.append((hit[0] | hit[1]).astype(BF16))
        mix = jnp.where(hit[0], gate[0:1], 0.0) + jnp.where(hit[1], gate[1:2], 0.0)
        slot_gate = slot_gate + jnp.sum(mix, axis=1, keepdims=True)
        upper_part = to_half(mix)
        mixes.append((upper_part, to_half(mix - upper_part.astype(F32))))

    def spread(mine):
        theirs = links.core_swap(mine)
        return dot(picks[0], mine) + dot(picks[1], theirs)

    cotangent = grad_out.reshape(tokens, width)
    upstream = cotangent.astype(F32)
    routed = to_half(spread(cotangent) * slot_gate)
    routed_in = links.exchange(routed, chunk)
    routed_all = links.gather_dp(routed_in)

    inputs = images.reshape(tokens, width).astype(F32)
    normal_one, inverse_one = normalize(inputs)
    normed_one = to_half(normal_one * gain_one + bias_one)
    normed_rel = dot_nt(normed_one, select).astype(BF16)
    bias_row = jnp.concatenate([full_q_bias, jnp.zeros((1, width), F32), full_v_bias], axis=1)
    projected = to_half(dot(normed_rel, qkv_rel) + bias_row)
    parts = projected.reshape(tokens, 3, heads, HEAD_DIM)
    queries, key_heads, value_heads = parts[:, 0], parts[:, 1], parts[:, 2]
    scores = head_scores(queries, key_heads)
    log_total = jnp.log(jnp.sum(jnp.exp(scores), axis=-1, keepdims=True))
    attention = to_half(jnp.exp(scores - log_total))
    context = jnp.einsum("hqk,khd->qhd", attention, value_heads, preferred_element_type=F32)
    context = to_half(context).reshape(tokens, width)
    out_full = dot_t(select, out_rel).astype(BF16)
    residual = inputs + dot(context, out_full) + full_out_bias
    normal_two, inverse_two = normalize(residual)
    normed_two = to_half(normal_two * gain_two + bias_two)

    received = links.exchange(spread(normed_two).astype(BF16), chunk)
    received_all = links.gather_dp(received)
    weight_in = in_weight[0]
    weight_down = down_weight[0]
    hidden_pre = dot(received, weight_in) + in_bias[0].astype(F32)
    grad_hidden = dot_nt(routed_in, weight_down)
    grad_pre = to_half(jax.vjp(jax.nn.gelu, hidden_pre)[1](grad_hidden)[0])
    grad_rows = dot_nt(grad_pre, weight_in).astype(BF16)
    grad_returned = links.exchange(grad_rows, chunk)
    activated = to_half(jax.nn.gelu(hidden_pre))
    expert_result = (dot(activated, weight_down) + down_bias[0].astype(F32)).astype(BF16)
    returned = links.exchange(expert_result, chunk)

    grad_normed_two = dot_t(picks[0], grad_returned) + links.core_swap(
        dot_t(picks[1], grad_returned)
    )
    ln2_gain_grad = jnp.sum(grad_normed_two * normal_two, axis=0)
    ln2_bias_grad = jnp.sum(grad_normed_two, axis=0)
    grad_residual = upstream + norm_back(grad_normed_two, normal_two, inverse_two, gain_two)
    out_bias_grad = jnp.sum(grad_residual, axis=0)
    branch_grad = to_half(grad_residual)
    half = width // 2
    context_rel = dot_nt(context, select).astype(BF16)
    out_share = links.scatter_sum(
        dot_t(context_rel[:, :half], branch_grad),
        dot_t(context_rel[:, half:], branch_grad).astype(BF16),
    )
    grad_context = to_half(dot_nt(branch_grad, out_full))
    probable = jnp.exp(head_scores(queries, key_heads) - log_total)
    incoming = grad_context.reshape(tokens, heads, HEAD_DIM)
    grad_values = jnp.einsum("hqk,qhd->khd", attention, incoming, preferred_element_type=F32)
    grad_probs = jnp.einsum("qhd,khd->hqk", incoming, value_heads, preferred_element_type=F32)
    centre = jnp.sum(probable * grad_probs, axis=-1, keepdims=True)
    grad_scores = to_half(probable * (grad_probs - centre) * HEAD_DIM ** (-0.5))
    grad_queries = jnp.einsum("hqk,khd->qhd", grad_scores, key_heads, preferred_element_type=F32)
    grad_keys = jnp.einsum("hqk,qhd->khd", grad_scores, queries, preferred_element_type=F32)
    grad_queries, grad_keys, grad_values = (
        part.reshape(tokens, width) for part in (grad_queries, grad_keys, grad_values)
    )
    q_bias_grad = jnp.sum(grad_queries, axis=0)
    v_bias_grad = jnp.sum(grad_values, axis=0)
    projected_grad = to_half(jnp.concatenate([grad_queries, grad_keys, grad_values], axis=1))
    qkv_share = links.scatter_sum(
        dot_t(normed_rel[:, :half], projected_grad),
        dot_t(normed_rel[:, half:], projected_grad).astype(BF16),
    )
    qkv_full = dot_t(select, qkv_rel).astype(BF16)
    grad_normed_one = dot_nt(projected_grad, qkv_full)
    ln1_gain_grad = jnp.sum(grad_normed_one * normal_one, axis=0)
    ln1_bias_grad = jnp.sum(grad_normed_one, axis=0)
    image_grad = (
        grad_residual + norm_back(grad_normed_one, normal_one, inverse_one, gain_one)
    ).reshape(images.shape)
    vector_grads = jnp.stack(
        [
            ln1_gain_grad,
            ln1_bias_grad,
            q_bias_grad,
            v_bias_grad,
            out_bias_grad,
            ln2_gain_grad,
            ln2_bias_grad,
        ]
    )
    vector_grads = jnp.pad(vector_grads, ((0, 128 - 7), (0, 0)))
    vector_rel = dot_nt(select, vector_grads.astype(BF16))
    vector_share = links.scatter_sum(vector_rel[:half], vector_rel[half:].astype(BF16))

    mixture = [dot_t(upper_part, returned) + dot_t(rest, returned) for upper_part, rest in mixes]
    block_output = (residual + (mixture[0] + links.core_swap(mixture[1]))).astype(BF16)

    dp_index = lax.axis_index("dp")
    share = weight_in.shape[1] // lax.axis_size("dp")
    in_share = lax.dynamic_slice_in_dim(weight_in, dp_index * share, share, axis=1)
    down_share = lax.dynamic_slice_in_dim(weight_down, dp_index * share, share, axis=0)
    in_bias_share = lax.dynamic_slice_in_dim(in_bias[0], dp_index * share, share)
    hidden_all = dot(received_all, in_share) + in_bias_share.astype(F32)
    activated_all = to_half(jax.nn.gelu(hidden_all))
    grad_all = to_half(
        jax.vjp(jax.nn.gelu, hidden_all)[1](dot_nt(routed_all, down_share))[0]
    )
    grad_weight_in = dot_t(received_all, grad_all)
    grad_weight_down = dot_t(activated_all, routed_all)
    grad_bias_in = jnp.sum(grad_all.astype(F32), axis=0)
    bias_share = width // lax.axis_size("dp")
    grad_bias_down = lax.dynamic_slice_in_dim(
        jnp.sum(routed_all.astype(F32), axis=0), dp_index * bias_share, bias_share
    )
    return (
        block_output.reshape(images.shape),
        image_grad,
        vector_share[:, 0],
        vector_share[:, 1],
        qkv_share,
        vector_share[:, 2],
        vector_share[:, 3],
        out_share,
        vector_share[:, 4],
        vector_share[:, 5],
        vector_share[:, 6],
        grad_weight_in[None],
        grad_bias_in[None],
        grad_weight_down[None],
        grad_bias_down[None],
    )


def solution(mesh):
    whole = P(BOTH)
    rows = P(BOTH, None)
    blocks = P(BOTH, None, None)
    in_specs = (
        blocks,
        whole,
        whole,
        rows,
        whole,
        whole,
        rows,
        whole,
        whole,
        whole,
        P("expert", None, None),
        P("expert", None),
        P("expert", None, None),
        P("expert", None),
        blocks,
        blocks,
        blocks,
    )
    out_specs = (
        blocks,
        blocks,
        whole,
        whole,
        rows,
        whole,
        whole,
        rows,
        whole,
        whole,
        whole,
        P("expert", None, "dp"),
        P("expert", "dp"),
        P("expert", "dp", None),
        P("expert", "dp"),
    )
    return jax.shard_map(
        per_device, mesh=mesh, in_specs=in_specs, out_specs=out_specs, check_vma=False
    )
```
